256 devices in a mesh: feat: 4 (over y), node: 64 (over x, z, core).
Axes of the slice: x: 4, y: 4, z: 8, core: 2. Of those that a mesh axis runs over, the one named last changes fastest.
Arguments:
- features: bfloat16 [64, 768, 2048], P('node', 'feat'), may hold values from -6 to 6
- tiles: bfloat16 [64, 48, 128, 128], P('node'), may hold values from -0.3125 to 0.3125
- tile_rows: int32 [64, 48], P('node'), may hold values from 0 to 15, as said below
- tile_cols: int32 [64, 48], P('node'), may hold values from 0 to 31
- send_rows: int32 [64, 64, 32], P('node'), may hold values from 0 to 2047, as said below
- send_count: int32 [64, 64], P('node'), may hold values from 0 to 32, as said below
- w_neigh: bfloat16 [768, 1024], P('feat'), may hold values from -0.15625 to 0.15625
- w_self: bfloat16 [768, 1024], P('feat'), may hold values from -0.15625 to 0.15625
- cotangent: bfloat16 [64, 2048, 1024], P('node', 'feat'), may hold values from -16 to 16
Outputs:
- hidden: bfloat16 [64, 2048, 1024], P('node', 'feat')
- grad_features: bfloat16 [64, 768, 2048], P('node', 'feat')
- grad_neigh: float32 [768, 1024], P('feat')
- grad_self: float32 [768, 1024], P('feat')
The draws below stay inside these ranges and needn't reach their ends.
Inputs may be any that keep to these rules, and one draw needn't show every extreme that they name: `tile_rows`: for each partition the first 16 tiles feed the row blocks 0, 1, 2 and so on in order, so that every block of rows has a tile. `send_rows`: rows may repeat within a list. `send_count`: A partition sends nothing to itself, and every partition fills all 32 slots toward at least one other partition.
All inputs are finite; a program needn't handle non-finite values.
Results may differ from the reference program's by a relative error of at most 0.0058.
Values may be sent and summed in bfloat16 or wider, within the bound.
A program may use at most 128 MiB of HBM per device.

```python
import jax
import jax.numpy as jnp
from jax import lax

F = 768
HID = 1024
TILE = 128
TILES_ROW = 3
HALO = 32
LOC = 2048
NPART = 64
EXT = 4096
K = 48
N_NODE = 64


def draw_tile_rows(key, part):
    blocks = LOC // TILE
    drawn = jax.random.randint(key, (NPART, K), 0, blocks).astype(jnp.int32)
    return drawn.at[:, :blocks].set(jnp.arange(blocks, dtype=jnp.int32)[None, :])


def draw_tile_cols(key, part):
    col_blocks = EXT // TILE
    drawn = jax.random.randint(key, (NPART, K), 0, col_blocks).astype(jnp.int32)
    drawn = drawn.at[0, 0].set(col_blocks - 1)
    return drawn.at[0, 1].set(0)


def draw_send_rows(key, part):
    drawn = jax.random.randint(key, (NPART, NPART, HALO), 0, LOC).astype(jnp.int32)
    drawn = drawn.at[0, 0, 0].set(0)
    return drawn.at[0, 0, 1].set(LOC - 1)


def draw_send_count(key, part):
    drawn = jax.random.randint(key, (NPART, NPART), 0, HALO + 1).astype(jnp.int32)
    idents = jnp.arange(NPART, dtype=jnp.int32)
    drawn = drawn.at[idents, (idents + 1) % NPART].set(HALO)
    return drawn.at[idents, idents].set(0)


def with_spikes(result, stream_key, source, target, blocks, factor):
    owner, partner = [(jnp.arange(result.shape[position]) // (result.shape[position] // blocks)).reshape([-1 if axis == position else 1 for axis in range(result.ndim)]) for position in (source, target)]
    chosen = jax.random.permutation(stream_key, blocks)[partner]
    strong = (owner == chosen) | (owner == (partner + blocks // 2) % blocks)
    return jnp.where(strong, factor * result, result)


def levels(own_key, extent, pieces, low, top_value):
    factor_of = 1.0
    for dim, shards_of in pieces:
        heights = jax.random.uniform(jax.random.fold_in(jax.random.fold_in(own_key, 6), dim), (shards_of,), jnp.float32, low / len(pieces), top_value / len(pieces))
        factor_of = factor_of * jnp.repeat(jnp.exp(heights), extent[dim] // shards_of).reshape((-1,) + (1,) * (len(extent) - 1 - dim))
    return factor_of


def noise(own_key, shape, deviation, limit, split=(), kind=jnp.bfloat16):
    values = deviation * jax.random.normal(own_key, shape, jnp.float32)
    if split:
        values = values * levels(own_key, shape, split, -0.22, 0.18)
    return jnp.clip(values, -limit, limit).astype(kind)


def noise_with(rng, extent, scale, reach, split, heavy, kind=jnp.bfloat16):
    array = scale * jax.random.normal(rng, extent, jnp.float32)
    if split:
        array = array * levels(rng, extent, split, -0.22, 0.18)
    return jnp.clip(with_spikes(array, jax.random.fold_in(rng, 3), *heavy), -reach, reach).astype(kind)


def setup_inputs(seed: int = 0) -> dict:
    arg_keys = jax.random.split(jax.random.key(seed), 10)
    features = noise(arg_keys[0], (NPART, F, LOC), 1.0, 6.0, ((0, 64), (1, 4)))
    tiles = noise(arg_keys[1], (NPART, K, TILE, TILE), (TILES_ROW * TILE) ** -0.5, 0.3125, ((0, 64),))
    tile_rows = draw_tile_rows(jax.random.fold_in(arg_keys[9], 71), 0)
    tile_cols = draw_tile_cols(jax.random.fold_in(arg_keys[9], 71), 0)
    send_rows = draw_send_rows(jax.random.fold_in(arg_keys[9], 71), 0)
    send_count = draw_send_count(jax.random.fold_in(arg_keys[9], 71), 0)
    w_neigh = noise(arg_keys[6], (F, HID), (2 * F) ** -0.5, 0.15625, ((0, 4),))
    w_self = noise(arg_keys[7], (F, HID), (2 * F) ** -0.5, 0.15625, ((0, 4),))
    cotangent = noise_with(arg_keys[8], (NPART, LOC, HID), 1.0, 16.0, ((0, 64), (1, 4)), (0, 2, 64, 4.0))
    return {"features": features, "tiles": tiles, "tile_rows": tile_rows, "tile_cols": tile_cols, "send_rows": send_rows, "send_count": send_count, "w_neigh": w_neigh, "w_self": w_self, "cotangent": cotangent}


def aggregate(extended, tile_vals, row_ids, col_ids):
    width = extended.shape[0]
    tile_side = tile_vals.shape[1]
    col_blocks = extended.shape[1] // tile_side
    gathered = extended.reshape(width, col_blocks, tile_side)[:, col_ids, :].astype(jnp.float32)
    partial_sums = jnp.einsum("fkj,kij->fki", gathered, tile_vals.astype(jnp.float32))
    onehot = (row_ids[:, None] == jnp.arange(LOC // TILE, dtype=jnp.int32)[None, :]).astype(jnp.float32)
    summed = jnp.einsum("fki,kr->fri", partial_sums, onehot, precision=lax.Precision.HIGHEST)
    return summed.reshape(width, LOC)


def spread_back(back_agg, tile_vals, row_ids, col_ids):
    width = back_agg.shape[0]
    tile_side = tile_vals.shape[1]
    blocks = back_agg.reshape(width, LOC // tile_side, tile_side)[:, row_ids, :].astype(jnp.float32)
    partial_sums = jnp.einsum("fki,kij->fkj", blocks, tile_vals.astype(jnp.float32))
    onehot = (col_ids[:, None] == jnp.arange(EXT // TILE, dtype=jnp.int32)[None, :]).astype(jnp.float32)
    summed = jnp.einsum("fkj,kc->fcj", partial_sums, onehot, precision=lax.Precision.HIGHEST)
    return summed.reshape(width, EXT)


def reference(features, tiles, tile_rows, tile_cols, send_rows, send_count, w_neigh, w_self, cotangent):
    parts = N_NODE
    live_slots = jnp.arange(HALO, dtype=jnp.int32)[None, None, :] < send_count[:, :, None]

    def incoming(part_id):
        index_rows = lax.dynamic_index_in_dim(send_rows, part_id, 1, keepdims=False)
        values = jax.vmap(lambda block, picks: block[:, picks])(features, index_rows)
        mask = lax.dynamic_index_in_dim(live_slots, part_id, 1, keepdims=False)[:, None, :]
        values = jnp.where(mask, values, jnp.zeros((), features.dtype))
        return jnp.transpose(values, (1, 0, 2)).reshape(F, parts * HALO)

    def one_part(carry, inputs):
        total_neigh, total_self = carry
        part_id, own_feats, tile_vals, row_ids, col_ids, cot_rows = inputs
        extended = jnp.concatenate([own_feats, incoming(part_id)], axis=1)
        aggregated = aggregate(extended, tile_vals, row_ids, col_ids).astype(jnp.bfloat16)
        preact = jnp.dot(aggregated.T, w_neigh, preferred_element_type=jnp.float32)
        preact = preact + jnp.dot(own_feats.T, w_self, preferred_element_type=jnp.float32)
        hidden = jax.nn.silu(preact).astype(jnp.bfloat16)
        gate_sig = jax.nn.sigmoid(preact)
        grad_pre = (cot_rows.astype(jnp.float32) * gate_sig * (1.0 + preact * (1.0 - gate_sig))).astype(jnp.bfloat16)
        total_neigh = total_neigh + jnp.dot(aggregated, grad_pre, preferred_element_type=jnp.float32)
        total_self = total_self + jnp.dot(own_feats, grad_pre, preferred_element_type=jnp.float32)
        back_agg = jnp.dot(w_neigh, grad_pre.T, preferred_element_type=jnp.float32).astype(jnp.bfloat16)
        back_self = jnp.dot(w_self, grad_pre.T, preferred_element_type=jnp.float32).astype(jnp.bfloat16)
        grad_ext = spread_back(back_agg, tile_vals, row_ids, col_ids)
        own_part = grad_ext[:, :LOC] + back_self.astype(jnp.float32)
        halo_part = grad_ext[:, LOC:]
        return (total_neigh, total_self), (hidden, own_part, halo_part)

    start = (jnp.zeros((F, HID), jnp.float32), jnp.zeros((F, HID), jnp.float32))
    part_ids = jnp.arange(parts, dtype=jnp.int32)
    sums, stacked = lax.scan(one_part, start, (part_ids, features, tiles, tile_rows, tile_cols, cotangent))
    hidden, own_parts, halo_parts = stacked

    def settle(inputs):
        part_id, own_part = inputs
        values = lax.dynamic_slice_in_dim(halo_parts, part_id * HALO, HALO, axis=2)
        mask = lax.dynamic_index_in_dim(live_slots, part_id, 0, keepdims=False)[:, None, :]
        values = jnp.where(mask, values, jnp.zeros((), values.dtype))
        values = jnp.transpose(values, (1, 0, 2)).reshape(F, parts * HALO)
        picks = lax.dynamic_index_in_dim(send_rows, part_id, 0, keepdims=False).reshape(-1)
        return own_part.at[:, picks].add(values).astype(jnp.bfloat16)

    grad_features = lax.map(settle, (part_ids, own_parts))
    grad_scale = float(LOC * N_NODE) ** -0.5
    return hidden, grad_features, sums[0] * grad_scale, sums[1] * grad_scale
```

```python
import functools

import jax
import jax.numpy as jnp
from jax import lax
from jax.experimental import pallas as pl
from jax.experimental.pallas import tpu as pltpu
from jax.sharding import PartitionSpec as P

NX, NY, NZ, NC = 4, 4, 8, 2
MESH = pl.DeviceIdType.MESH


def place():
    n = lax.axis_index("node")
    y = lax.axis_index("feat")
    return lax.div(n, NZ * NC), y, lax.rem(lax.div(n, NC), NZ), lax.rem(n, NC)


def node_id(x, z, c):
    return {"node": (x * NZ + z) * NC + c}


def remote(src, dst, send, recv, device):
    return pltpu.make_async_remote_copy(
        src_ref=src, dst_ref=dst, send_sem=send, recv_sem=recv, device_id=device, device_id_type=MESH
    )


def total_kernel(
    scale, term_ref, out_ref,
    core_in, sum1, y_in, sum2, x_in, sum3, z_in, sum4, strip, rows, other,
    core_sem, y_send, y_recv, x_send, x_recv, z_send, z_recv, zg_send, zg_recv, xg_send, xg_recv, cg_sem,
):
    x, y, z, c = place()
    feat = out_ref.shape[1]
    xr = feat // NX
    zc = out_ref.shape[2] // NZ
    partner = node_id(x, z, 1 - c)
    y_peer = lambda d: {"feat": lax.rem(y + d, NY)}
    x_peer = lambda d: node_id(lax.rem(x + d, NX), z, c)
    z_peer = lambda d: node_id(x, lax.rem(z + d, NZ), c)

    barrier = pltpu.get_barrier_semaphore()
    pl.semaphore_signal(barrier, inc=1, device_id=partner, device_id_type=MESH)
    for d in range(1, NY):
        pl.semaphore_signal(barrier, inc=1, device_id=y_peer(d), device_id_type=MESH)
    for d in range(1, NX):
        pl.semaphore_signal(barrier, inc=1, device_id=x_peer(d), device_id_type=MESH)
    for d in range(1, NZ):
        pl.semaphore_signal(barrier, inc=1, device_id=z_peer(d), device_id_type=MESH)
    pl.semaphore_wait(barrier, 1 + NY - 1 + NX - 1 + NZ - 1)

    f32 = jnp.float32
    bf16 = jnp.bfloat16
    swap = remote(term_ref.at[1 - c], core_in, core_sem.at[0], core_sem.at[1], partner)
    swap.start()
    swap.wait()

    y_copies = []
    for d in range(1, NY):
        q = lax.rem(y + d, NY)
        sum1[q] = (term_ref[c, q].astype(f32) + core_in[q].astype(f32)).astype(bf16)
        cp = remote(sum1.at[q], y_in.at[d - 1], y_send.at[d - 1], y_recv.at[d - 1], y_peer(d))
        cp.start()
        y_copies.append(cp)
    acc = term_ref[c, y].astype(f32) + core_in[y].astype(f32)
    for cp in y_copies:
        cp.wait()
    for d in range(1, NY):
        acc = acc + y_in[d - 1].astype(f32)
    acc = acc.reshape(NX, xr, acc.shape[1])
    sum2[...] = acc.astype(bf16)

    x_copies = []
    for d in range(1, NX):
        q = lax.rem(x + d, NX)
        cp = remote(sum2.at[q], x_in.at[d - 1], x_send.at[d - 1], x_recv.at[d - 1], x_peer(d))
        cp.start()
        x_copies.append(cp)
    for cp in x_copies:
        cp.wait()
    acc = sum2[x].astype(f32)
    for d in range(1, NX):
        acc = acc + x_in[d - 1].astype(f32)
    for q in range(NZ):
        sum3[q] = acc[:, q * zc:(q + 1) * zc].astype(bf16)

    z_copies = []
    for d in range(1, NZ):
        q = lax.rem(z + d, NZ)
        cp = remote(sum3.at[q], z_in.at[d - 1], z_send.at[d - 1], z_recv.at[d - 1], z_peer(d))
        cp.start()
        z_copies.append(cp)
    for cp in z_copies:
        cp.wait()
    acc = sum3[z].astype(f32)
    for d in range(1, NZ):
        acc = acc + z_in[d - 1].astype(f32)
    sum4[...] = acc.astype(bf16)

    z_copies = []
    for d in range(1, NZ):
        cp = remote(sum4, strip.at[z], zg_send.at[d - 1], zg_recv.at[d - 1], z_peer(d))
        cp.start()
        z_copies.append(cp)
    strip[z] = sum4[...]
    for cp in z_copies:
        cp.wait()

    x_copies = []
    for d in range(1, NX):
        cp = remote(strip, rows.at[x], xg_send.at[d - 1], xg_recv.at[d - 1], x_peer(d))
        cp.start()
        x_copies.append(cp)
    rows[x] = strip[...]
    for cp in x_copies:
        cp.wait()

    back = remote(rows, other, cg_sem.at[0], cg_sem.at[1], partner)
    back.start()
    for a in range(NX):
        for b in range(NZ):
            out_ref[c, a * xr:(a + 1) * xr, b * zc:(b + 1) * zc] = rows[a, b].astype(f32) * scale
    back.wait()
    for a in range(NX):
        for b in range(NZ):
            out_ref[1 - c, a * xr:(a + 1) * xr, b * zc:(b + 1) * zc] = other[a, b].astype(f32) * scale


def total_grads(terms, scale):
    _, parts, feat, hid = terms.shape
    xr, zc = feat // NX, hid // NZ
    bf16 = jnp.bfloat16
    dma = pltpu.SemaphoreType.DMA
    return pl.pallas_call(
        functools.partial(total_kernel, scale),
        out_shape=jax.ShapeDtypeStruct((NC, feat, hid), jnp.float32),
        in_specs=[pl.BlockSpec(memory_space=pltpu.VMEM)],
        out_specs=pl.BlockSpec(memory_space=pltpu.VMEM),
        scratch_shapes=[
            pltpu.VMEM((parts, feat, hid), bf16),
            pltpu.VMEM((parts, feat, hid), bf16),
            pltpu.VMEM((NY - 1, feat, hid), bf16),
            pltpu.VMEM((NX, xr, hid), bf16),
            pltpu.VMEM((NX - 1, xr, hid), bf16),
            pltpu.VMEM((NZ, xr, zc), bf16),
            pltpu.VMEM((NZ - 1, xr, zc), bf16),
            pltpu.VMEM((xr, zc), bf16),
            pltpu.VMEM((NZ, xr, zc), bf16),
            pltpu.VMEM((NX, NZ, xr, zc), bf16),
            pltpu.VMEM((NX, NZ, xr, zc), bf16),
            dma((2,)), dma((NY - 1,)), dma((NY - 1,)), dma((NX - 1,)), dma((NX - 1,)),
            dma((NZ - 1,)), dma((NZ - 1,)), dma((NZ - 1,)), dma((NZ - 1,)),
            dma((NX - 1,)), dma((NX - 1,)), dma((2,)),
        ],
        compiler_params=pltpu.CompilerParams(
            collective_id=0, has_side_effects=True, vmem_limit_bytes=48 << 20
        ),
        name="total_grads",
    )(terms)


def per_device(
    features, tiles, tile_rows, tile_cols, send_rows, send_count, w_neigh, w_self, cotangent
):
    own_cols = features[0]
    feat_dev, own_rows = own_cols.shape
    tile_vals = tiles[0]
    tile_side = tile_vals.shape[1]
    row_ids = tile_rows[0]
    col_ids = tile_cols[0]
    targets = send_rows[0]
    amounts = send_count[0]
    parts, slots = targets.shape
    live_slots = lax.broadcasted_iota(jnp.int32, (parts, slots), 1) < amounts[:, None]
    picked = jnp.take(own_cols, targets.reshape(-1), axis=1).reshape(feat_dev, parts, slots)
    picked = jnp.where(live_slots[None], picked, jnp.zeros((), own_cols.dtype))
    arrived = lax.all_to_all(picked, "node", split_axis=1, concat_axis=1, tiled=True)
    extended = jnp.concatenate([own_cols, arrived.reshape(feat_dev, parts * slots)], axis=1)
    col_blocks = extended.shape[1] // tile_side
    row_blocks = own_rows // tile_side
    gathered_cols = extended.reshape(feat_dev, col_blocks, tile_side)[:, col_ids, :]
    partial_sums = jnp.einsum(
        "fkj,kij->fki", gathered_cols, tile_vals, preferred_element_type=jnp.float32
    )
    row_onehot = (row_ids[:, None] == lax.broadcasted_iota(jnp.int32, (1, row_blocks), 1)).astype(
        jnp.float32
    )
    aggregated = jnp.einsum(
        "fki,kr->fri", partial_sums, row_onehot, precision=lax.Precision.HIGHEST
    )
    aggregated = aggregated.reshape(feat_dev, own_rows).astype(jnp.bfloat16)
    full_neigh, full_self = (
        lax.all_gather(w_neigh, "feat", axis=0, tiled=True),
        lax.all_gather(w_self, "feat", axis=0, tiled=True),
    )
    agg_rows, self_rows = (
        lax.all_to_all(aggregated, "feat", split_axis=1, concat_axis=0, tiled=True),
        lax.all_to_all(own_cols, "feat", split_axis=1, concat_axis=0, tiled=True),
    )
    first_dims = (((0,), (0,)), ((), ()))
    preact = lax.dot_general(agg_rows, full_neigh, first_dims, preferred_element_type=jnp.float32)
    preact = preact + lax.dot_general(
        self_rows, full_self, first_dims, preferred_element_type=jnp.float32
    )
    hidden = jax.nn.silu(preact).astype(jnp.bfloat16)
    gate_sig = jax.nn.sigmoid(preact)
    grad_pre = (
        cotangent[0].astype(jnp.float32) * gate_sig * (1.0 + preact * (1.0 - gate_sig))
    ).astype(jnp.bfloat16)
    grad_scale = float(own_rows * lax.axis_size("node")) ** (-0.5)
    last_dims = (((1,), (1,)), ((), ()))
    term_neigh = jnp.dot(agg_rows, grad_pre, preferred_element_type=jnp.float32)
    term_self = jnp.dot(self_rows, grad_pre, preferred_element_type=jnp.float32)
    terms = jnp.stack([term_neigh.astype(jnp.bfloat16), term_self.astype(jnp.bfloat16)])
    totals = total_grads(terms.reshape(NC, NY, feat_dev, terms.shape[-1]), grad_scale)
    back_agg = lax.dot_general(
        full_neigh, grad_pre, last_dims, preferred_element_type=jnp.float32
    ).astype(jnp.bfloat16)
    back_self = lax.dot_general(
        full_self, grad_pre, last_dims, preferred_element_type=jnp.float32
    ).astype(jnp.bfloat16)
    grad_agg, grad_own = (
        lax.all_to_all(back_agg, "feat", split_axis=0, concat_axis=1, tiled=True),
        lax.all_to_all(back_self, "feat", split_axis=0, concat_axis=1, tiled=True),
    )
    grad_blocks = grad_agg.reshape(feat_dev, row_blocks, tile_side)[:, row_ids, :]
    spread = jnp.einsum("fki,kij->fkj", grad_blocks, tile_vals, preferred_element_type=jnp.float32)
    col_onehot = (col_ids[:, None] == lax.broadcasted_iota(jnp.int32, (1, col_blocks), 1)).astype(
        jnp.float32
    )
    grad_ext = jnp.einsum("fkj,kc->fcj", spread, col_onehot, precision=lax.Precision.HIGHEST)
    grad_ext = grad_ext.reshape(feat_dev, col_blocks * tile_side)
    outgoing = grad_ext[:, own_rows:].reshape(feat_dev, parts, slots)
    returned = lax.all_to_all(outgoing, "node", split_axis=1, concat_axis=1, tiled=True)
    returned = jnp.where(live_slots[None], returned, jnp.zeros((), returned.dtype))
    grad_cols = grad_ext[:, :own_rows] + grad_own.astype(jnp.float32)
    grad_cols = grad_cols.at[:, targets.reshape(-1)].add(returned.reshape(feat_dev, parts * slots))
    return (
        hidden[None],
        grad_cols.astype(jnp.bfloat16)[None],
        totals[0],
        totals[1],
    )


def solution(mesh):
    placed = (
        P("node", "feat", None),
        P("node", None, None, None),
        P("node", None),
        P("node", None),
        P("node", None, None),
        P("node", None),
        P("feat", None),
        P("feat", None),
        P("node", "feat", None),
    )
    return jax.shard_map(
        per_device,
        mesh=mesh,
        in_specs=placed,
        out_specs=(
            P("node", "feat", None),
            P("node", "feat", None),
            P("feat", None),
            P("feat", None),
        ),
        check_vma=False,
    )
```

```python
import functools

import jax
import jax.numpy as jnp
from jax import lax
from jax.experimental import pallas as pl
from jax.experimental.pallas import tpu as pltpu
from jax.sharding import PartitionSpec as P

NX, NY, NZ, NC = 4, 4, 8, 2
NODES = NX * NZ * NC
GROUP = NZ * NC
X_ORDER = (2, 1, 3, 0)
MESH = pl.DeviceIdType.MESH
F32 = jnp.float32
BF16 = jnp.bfloat16
CONTRACT_FIRST = (((0,), (0,)), ((), ()))
CONTRACT_LAST = (((1,), (1,)), ((), ()))


def node_of(x, z, c):
    return (x * NZ + z) * NC + c


def remote(src, dst, send, recv, device):
    return pltpu.make_async_remote_copy(
        src_ref=src, dst_ref=dst, send_sem=send, recv_sem=recv, device_id=device, device_id_type=MESH
    )


def dot(a, b):
    return jnp.dot(a, b, preferred_element_type=F32)


def dot_last(a, b):
    return lax.dot_general(a, b, CONTRACT_LAST, preferred_element_type=F32)


def exchange_quarters(pieces):
    quarter = pieces[0].shape[1] // 4
    lane_quarter = lax.broadcasted_iota(jnp.int32, pieces[0].shape, 1) // quarter
    result = []
    for b in range(4):
        moved = pieces[b]
        for a in range(4):
            if a != b:
                rolled = pltpu.roll(pieces[a], ((a - b) % 4) * quarter, 1)
                moved = jnp.where(lane_quarter == a, rolled, moved)
        result.append(moved)
    return result


def layer_kernel(
    scale,
    table, picks, feat_hbm, tiles_hbm, wn_hbm, ws_hbm, cot_hbm,
    hidden_hbm, gfeat_ref, total_ref,
    feat, tiles, cot, weights, onehot, msg_out, msg_in, ext, running, agg_out, cols, pre, gate, hidden,
    back_out, back_in, own_term, other_term, core_in, x_out, x_in, y_out, y_in, z_out, z_in, z_sum,
    strip, rows, other, blocks, spread, acc,
    ret_out, ret_in,
    load_sem, halo_send, halo_recv, self_send, self_recv, w_send, w_recv, wf_send, wf_recv, wc_send, wc_recv,
    agg_send, agg_recv, ba_send, ba_recv, bs_send, bs_recv, c_send, c_recv, x_send, x_recv, y_send, y_recv,
    z_send, z_recv, zg_send, zg_recv, xg_send, xg_recv, cg_send, cg_recv, ret_send, ret_recv,
):
    n = lax.axis_index("node")
    y = lax.axis_index("feat")
    x, z, c = lax.div(n, GROUP), lax.rem(lax.div(n, NC), NZ), lax.rem(n, NC)
    partner = {"node": node_of(x, z, 1 - c)}
    y_of = lambda d: lax.rem(y + d, NY)
    x_of = lambda d: lax.rem(x + d, NX)
    z_of = lambda d: lax.rem(z + d, NZ)
    c_of = lambda d: lax.rem(c + d, NC)
    y_peer = lambda d: {"feat": y_of(d)}
    x_peer = lambda d: {"node": node_of(x_of(d), z, c)}
    z_peer = lambda d: {"node": node_of(x, z_of(d), c)}
    width, own_rows = feat.shape
    share = own_rows // NY
    side = tiles.shape[1]
    n_tiles = tiles.shape[0]
    own_blocks = own_rows // side
    lanes = GROUP * 32
    hid = gate.shape[1]
    xr, zc = width // NX, hid // NZ
    offsets = [(dx, dz, dc) for dx in X_ORDER for dz in range(NZ) for dc in range(NC) if dx or dz or dc]

    barrier = pltpu.get_barrier_semaphore()
    for dx, dz, dc in offsets:
        pl.semaphore_signal(
            barrier, inc=1, device_id={"node": node_of(x_of(dx), z_of(dz), c_of(dc))}, device_id_type=MESH
        )
    for d in range(1, NY):
        pl.semaphore_signal(barrier, inc=1, device_id=y_peer(d), device_id_type=MESH)

    loads = [
        pltpu.make_async_copy(feat_hbm, feat, load_sem.at[0]),
        pltpu.make_async_copy(wn_hbm, weights.at[0, y], load_sem.at[1]),
        pltpu.make_async_copy(ws_hbm, weights.at[1, y], load_sem.at[2]),
        pltpu.make_async_copy(tiles_hbm, tiles, load_sem.at[3]),
        pltpu.make_async_copy(cot_hbm, cot, load_sem.at[4]),
    ]
    for load in loads:
        load.start()
    loads[0].wait()
    msg_in[n] = jnp.zeros(msg_in.shape[1:], BF16)

    def pick(dx):
        part = x_of(dx)
        wanted = picks[part]
        ids = lax.broadcasted_iota(jnp.int32, (own_rows, lanes), 0)
        onehot[part] = jnp.where(ids == wanted, 1.0, 0.0).astype(BF16)
        picked = dot(feat[...], onehot[part])
        for b in range(lanes // side):
            block = picked[:, b * side:(b + 1) * side]
            height = width // 4
            moved = exchange_quarters([block[a * height:(a + 1) * height] for a in range(4)])
            for p in range(4):
                msg_out[part * GROUP + b * 4 + p] = moved[p].astype(BF16)

    def halo_copies(dx, out, into, send, recv):
        result = []
        for dz in range(NZ):
            for dc in range(NC):
                if dx or dz or dc:
                    o = (dx * NZ + dz) * NC + dc
                    peer = node_of(x_of(dx), z_of(dz), c_of(dc))
                    result.append(remote(out.at[peer], into.at[n], send.at[o], recv.at[o], {"node": peer}))
        return result

    def halo_waits(dx, out, into, send, recv):
        for dz in range(NZ):
            for dc in range(NC):
                if dx or dz or dc:
                    o = (dx * NZ + dz) * NC + dc
                    src = node_of(x_of(NX - dx), z_of(NZ - dz), c_of(NC - dc))
                    remote(out.at[src], into.at[src], send.at[o], recv.at[o], {"node": src}).wait_recv()

    pick(X_ORDER[0])
    pl.semaphore_wait(barrier, len(offsets) + NY - 1)
    halo = halo_copies(X_ORDER[0], msg_out, msg_in, halo_send, halo_recv)
    for cp in halo:
        cp.start()
    loads[1].wait()
    loads[2].wait()
    w_right = remote(weights.at[c, y], weights.at[c, y], w_send.at[0], w_recv.at[0], y_peer(1))
    w_left = remote(weights.at[c, y], weights.at[c, y], w_send.at[1], w_recv.at[1], y_peer(NY - 1))
    w_right.start()
    w_left.start()
    selfs = []
    for d in range(1, NY):
        q = y_of(d)
        cp = remote(
            feat_hbm.at[:, pl.ds(pl.multiple_of(q * share, share), share)], cols.at[1, y],
            self_send.at[d - 1], self_recv.at[d - 1], y_peer(d),
        )
        cp.start()
        selfs.append(cp)
    cols[1, y] = feat[:, pl.ds(pl.multiple_of(y * share, share), share)]
    for dx in X_ORDER[1:]:
        pick(dx)
        more = halo_copies(dx, msg_out, msg_in, halo_send, halo_recv)
        for cp in more:
            cp.start()
        halo = halo + more

    half = width // 2
    low, high = pl.ds(0, half), pl.ds(half, half)
    left_id, right_id, far_id = y_of(NY - 1), y_of(1), y_of(2)
    w_right.wait_recv()
    w_far_right = remote(
        weights.at[c, left_id, low], weights.at[c, left_id, low], wf_send.at[0], wf_recv.at[0], y_peer(1)
    )
    w_far_right.start()
    w_left.wait_recv()
    w_far_left = remote(
        weights.at[c, right_id, high], weights.at[c, right_id, high], wf_send.at[1], wf_recv.at[1], y_peer(NY - 1)
    )
    w_far_left.start()
    w_core = []
    for i, q in enumerate((left_id, right_id, far_id)):
        if i == 2:
            w_far_right.wait_recv()
            w_far_left.wait_recv()
        cp = remote(weights.at[c, q], weights.at[c, q], wc_send.at[i], wc_recv.at[i], partner)
        cp.start()
        w_core.append(cp)

    for b in range(own_blocks):
        ext[b] = feat[:, b * side:(b + 1) * side]
    loads[3].wait()
    height = width // 4

    def unpack(source, first):
        moved = exchange_quarters([source[first + p].astype(F32) for p in range(4)])
        return jnp.concatenate([piece.astype(BF16) for piece in moved], axis=0)

    for dx in X_ORDER:
        halo_waits(dx, msg_out, msg_in, halo_send, halo_recv)
        part = x_of(NX - dx)
        for b in range(GROUP // 4):
            ext[own_blocks + part * (GROUP // 4) + b] = unpack(msg_in, part * GROUP + b * 4)

    unroll = 4

    def aggregate(i, total):
        for u in range(unroll):
            s = i * unroll + u
            total = total * table[2, s].astype(F32) + dot_last(ext[table[1, s]], tiles[table[0, s]])
            running[s] = total.astype(BF16)
        return total

    lax.fori_loop(0, n_tiles // unroll, aggregate, jnp.zeros((width, side), F32))
    per = own_blocks // NY
    for r in range(own_blocks):
        agg_out[r // per, :, (r % per) * side:(r % per + 1) * side] = running[table[3, r]]
    aggs = []
    for d in range(1, NY):
        cp = remote(agg_out.at[y_of(d)], cols.at[0, y], agg_send.at[d - 1], agg_recv.at[d - 1], y_peer(d))
        cp.start()
        aggs.append(cp)
    cols[0, y] = agg_out[y]

    for cp in selfs:
        cp.wait_recv()
    for cp in w_core:
        cp.wait_recv()
    strips = 4
    wide = hid // strips

    def self_part(i, carry):
        at = pl.ds(pl.multiple_of(i * wide, wide), wide)
        left = cols[1].reshape(NY * width, share)
        right = weights[1, :, :, at].reshape(NY * width, wide)
        pre[:, at] = lax.dot_general(left, right, CONTRACT_FIRST, preferred_element_type=F32)
        return carry

    lax.fori_loop(0, strips, self_part, 0)
    loads[4].wait()
    for cp in aggs:
        cp.wait_recv()

    def neigh_part(i, carry):
        at = pl.ds(pl.multiple_of(i * wide, wide), wide)
        left = cols[0].reshape(NY * width, share)
        right = weights[0, :, :, at].reshape(NY * width, wide)
        value = pre[:, at] + lax.dot_general(left, right, CONTRACT_FIRST, preferred_element_type=F32)
        sig = jax.nn.sigmoid(value)
        hidden[:, at] = (value * sig).astype(BF16)
        gate[:, at] = (cot[:, at].astype(F32) * sig * (1.0 + value * (1.0 - sig))).astype(BF16)
        return carry

    lax.fori_loop(0, strips, neigh_part, 0)
    store_hidden = pltpu.make_async_copy(hidden, hidden_hbm, load_sem.at[5])
    store_hidden.start()

    backs = []
    for d in range(1, NY):
        q = y_of(d)
        back_out[0, q] = dot_last(weights[0, q], gate[...]).astype(BF16)
        cp = remote(back_out.at[0, q], back_in.at[0, y], ba_send.at[d - 1], ba_recv.at[d - 1], y_peer(d))
        cp.start()
        backs.append(cp)
    back_in[0, y] = dot_last(weights[0, y], gate[...]).astype(BF16)

    swaps = []
    for q in range(NY):
        other_term[q] = dot(cols[1 - c, q], gate[...]).astype(BF16)
        cp = remote(other_term.at[q], core_in.at[q], c_send.at[q], c_recv.at[q], partner)
        cp.start()
        swaps.append(cp)
    for q in range(NY):
        own_term[q] = dot(cols[c, q], gate[...])
    back_selfs = []
    for d in range(1, NY):
        q = y_of(d)
        back_out[1, q] = dot_last(weights[1, q], gate[...]).astype(BF16)
        cp = remote(back_out.at[1, q], back_in.at[1, y], bs_send.at[d - 1], bs_recv.at[d - 1], y_peer(d))
        cp.start()
        back_selfs.append(cp)
    back_in[1, y] = dot_last(weights[1, y], gate[...]).astype(BF16)

    for q in range(NY):
        swaps[q].wait_recv()
        for a in range(NX):
            at = slice(a * xr, (a + 1) * xr)
            both = own_term[q, at] + core_in[q, at].astype(F32)
            own_term[q, at] = both
            x_out[a, q] = both.astype(BF16)
    xs = []
    for d in range(1, NX):
        cp = remote(x_out.at[x_of(d)], x_in.at[d - 1], x_send.at[d - 1], x_recv.at[d - 1], x_peer(d))
        cp.start()
        xs.append(cp)

    for cp in backs:
        cp.wait_recv()
    for r in range(own_blocks):
        blocks[r] = back_in[0, r // per, :, (r % per) * side:(r % per + 1) * side]

    def spread_back(i, total):
        for u in range(unroll):
            s = i * unroll + u
            total = total * table[6, s].astype(F32) + dot(blocks[table[5, s]], tiles[table[4, s]])
            spread[s] = total
        return total

    lax.fori_loop(0, n_tiles // unroll, spread_back, jnp.zeros((width, side), F32))
    returns = []
    for dx in X_ORDER:
        part = x_of(dx)
        for b in range(GROUP // 4):
            col = own_blocks + part * (GROUP // 4) + b
            block = spread[table[7, col]] * table[8, col].astype(F32)
            moved = exchange_quarters([block[a * height:(a + 1) * height] for a in range(4)])
            for p in range(4):
                ret_out[part * GROUP + b * 4 + p] = moved[p].astype(BF16)
        more = halo_copies(dx, ret_out, ret_in, ret_send, ret_recv)
        for cp in more:
            cp.start()
        returns = returns + more
    ret_in[n] = jnp.zeros(ret_in.shape[1:], BF16)

    for cp in xs:
        cp.wait_recv()
    mine = own_term[:, pl.ds(pl.multiple_of(x * xr, xr), xr), :]
    for d in range(1, NX):
        mine = mine + x_in[d - 1].astype(F32)
    for q in range(NY):
        y_out[q] = mine[q].astype(BF16)
    ys = []
    for d in range(1, NY):
        cp = remote(y_out.at[y_of(d)], y_in.at[d - 1], y_send.at[d - 1], y_recv.at[d - 1], y_peer(d))
        cp.start()
        ys.append(cp)

    for cp in back_selfs:
        cp.wait_recv()
    for b in range(own_blocks):
        at = slice(b * side, (b + 1) * side)
        inner = slice((b % per) * side, (b % per + 1) * side)
        acc[:, at] = spread[table[7, b]] * table[8, b].astype(F32) + back_in[1, b // per, :, inner].astype(F32)

    for cp in ys:
        cp.wait_recv()
    mine = y_out[y].astype(F32)
    for d in range(1, NY):
        mine = mine + y_in[d - 1].astype(F32)
    for q in range(NZ):
        z_out[q] = mine[:, q * zc:(q + 1) * zc].astype(BF16)
    zs = []
    for d in range(1, NZ):
        cp = remote(z_out.at[z_of(d)], z_in.at[d - 1], z_send.at[d - 1], z_recv.at[d - 1], z_peer(d))
        cp.start()
        zs.append(cp)
    for cp in zs:
        cp.wait_recv()
    mine = z_out[z].astype(F32)
    for d in range(1, NZ):
        mine = mine + z_in[d - 1].astype(F32)
    z_sum[...] = mine.astype(BF16)
    zgs = []
    for d in range(1, NZ):
        cp = remote(z_sum, strip.at[z], zg_send.at[d - 1], zg_recv.at[d - 1], z_peer(d))
        cp.start()
        zgs.append(cp)
    strip[z] = z_sum[...]
    for cp in zgs:
        cp.wait_recv()
    xgs = []
    for d in range(1, NX):
        cp = remote(strip, rows.at[x], xg_send.at[d - 1], xg_recv.at[d - 1], x_peer(d))
        cp.start()
        xgs.append(cp)
    rows[x] = strip[...]

    def scatter(dx):
        halo_waits(dx, ret_out, ret_in, ret_send, ret_recv)
        part = x_of(NX - dx)
        came = jnp.concatenate(
            [unpack(ret_in, part * GROUP + b * 4) for b in range(GROUP // 4)], axis=1
        )
        acc[...] += dot_last(came, onehot[part])

    scatter(X_ORDER[0])
    for cp in xgs:
        cp.wait_recv()
    last = remote(rows, other, cg_send.at[0], cg_recv.at[0], partner)
    last.start()
    for dx in X_ORDER[1:]:
        scatter(dx)
    gfeat_ref[...] = acc[...].astype(BF16)
    last.wait_recv()
    for a in range(NX):
        for b in range(NZ):
            ra, cb = slice(a * xr, (a + 1) * xr), slice(b * zc, (b + 1) * zc)
            total_ref[c, ra, cb] = rows[a, b].astype(F32) * scale
            total_ref[1 - c, ra, cb] = other[a, b].astype(F32) * scale
    store_hidden.wait()
    for cp in (
        halo + selfs + [w_right, w_left, w_far_right, w_far_left] + w_core + aggs + backs + swaps + back_selfs
        + xs + returns + ys + zs + zgs + xgs + [last]
    ):
        cp.wait_send()


def layer(table, picks, feat, tiles, wn, ws, cot, scale):
    width, own_rows = feat.shape
    n_tiles, side, _ = tiles.shape
    share, hid = cot.shape
    xr, zc = width // NX, hid // NZ
    own_blocks = own_rows // side
    lanes = own_rows // NX
    height = width // 4
    vmem = pltpu.VMEM
    dma = lambda k: pltpu.SemaphoreType.DMA((k,))
    any_space = pl.BlockSpec(memory_space=pl.ANY)
    in_vmem = pl.BlockSpec(memory_space=pltpu.VMEM)
    return pl.pallas_call(
        functools.partial(layer_kernel, scale),
        out_shape=(
            jax.ShapeDtypeStruct((share, hid), BF16),
            jax.ShapeDtypeStruct((width, own_rows), BF16),
            jax.ShapeDtypeStruct((NC, width, hid), F32),
        ),
        in_specs=[pl.BlockSpec(memory_space=pltpu.SMEM), in_vmem] + [any_space] * 5,
        out_specs=(any_space, in_vmem, in_vmem),
        scratch_shapes=[
            vmem((width, own_rows), BF16),
            vmem((n_tiles, side, side), BF16),
            vmem((share, hid), BF16),
            vmem((2, NY, width, hid), BF16),
            vmem((NX, own_rows, lanes), BF16),
            vmem((NODES, height, side), BF16),
            vmem((NODES, height, side), BF16),
            vmem((2 * own_blocks, width, side), BF16),
            vmem((n_tiles, width, side), BF16),
            vmem((NY, width, share), BF16),
            vmem((2, NY, width, share), BF16),
            vmem((share, hid), F32),
            vmem((share, hid), BF16),
            vmem((share, hid), BF16),
            vmem((2, NY, width, share), BF16),
            vmem((2, NY, width, share), BF16),
            vmem((NY, width, hid), F32),
            vmem((NY, width, hid), BF16),
            vmem((NY, width, hid), BF16),
            vmem((NX, NY, xr, hid), BF16),
            vmem((NX - 1, NY, xr, hid), BF16),
            vmem((NY, xr, hid), BF16),
            vmem((NY - 1, xr, hid), BF16),
            vmem((NZ, xr, zc), BF16),
            vmem((NZ - 1, xr, zc), BF16),
            vmem((xr, zc), BF16),
            vmem((NZ, xr, zc), BF16),
            vmem((NX, NZ, xr, zc), BF16),
            vmem((NX, NZ, xr, zc), BF16),
            vmem((own_blocks, width, side), BF16),
            vmem((n_tiles, width, side), F32),
            vmem((width, own_rows), F32),
            vmem((NODES, height, side), BF16),
            vmem((NODES, height, side), BF16),
            dma(6), dma(NODES), dma(NODES), dma(3), dma(3), dma(2), dma(2), dma(2), dma(2), dma(3), dma(3),
            dma(3), dma(3), dma(3), dma(3), dma(3), dma(3), dma(4), dma(4), dma(3), dma(3), dma(3), dma(3),
            dma(7), dma(7), dma(7), dma(7), dma(3), dma(3), dma(1), dma(1), dma(NODES), dma(NODES),
        ],
        compiler_params=pltpu.CompilerParams(
            collective_id=0, has_side_effects=True, vmem_limit_bytes=60 << 20
        ),
        name="sage_layer",
    )(table, picks, feat, tiles, wn, ws, cot)


def tile_order(row_ids, col_ids, col_blocks):
    count = row_ids.shape[0]
    keys = jnp.stack([row_ids, col_ids])
    place = lax.broadcasted_iota(jnp.int32, (count,), 0)
    before = (keys[:, None, :] < keys[:, :, None]) | (
        (keys[:, None, :] == keys[:, :, None]) & (place[None, None, :] < place[None, :, None])
    )
    rank = jnp.sum(before.astype(jnp.int32), axis=2)
    chosen = (rank[:, None, :] == place[None, :, None]).astype(jnp.int32)
    order = jnp.sum(chosen * place[None, None, :], axis=2)
    own = jnp.sum(chosen * keys[:, None, :], axis=2)
    across = jnp.sum(chosen * keys[::-1][:, None, :], axis=2)
    earlier = jnp.concatenate([jnp.full((2, 1), -1, jnp.int32), own[:, :-1]], axis=1)
    keep = (own == earlier).astype(jnp.int32)
    ids = lax.broadcasted_iota(jnp.int32, (count,), 0)
    upto = jnp.sum((keys[:, None, :] <= ids[None, :, None]).astype(jnp.int32), axis=2)
    has = jnp.sum((keys[:, None, :] == ids[None, :, None]).astype(jnp.int32), axis=2) > 0
    last = jnp.maximum(upto - 1, 0)
    return jnp.stack(
        [order[0], across[0], keep[0], last[0], order[1], across[1], keep[1], last[1], has[1].astype(jnp.int32)]
    )


def per_device(
    features, tiles, tile_rows, tile_cols, send_rows, send_count, w_neigh, w_self, cotangent
):
    own_rows = features.shape[2]
    parts, slots = send_rows.shape[1:]
    live = lax.broadcasted_iota(jnp.int32, (parts, slots), 1) < send_count[0][:, None]
    picks = jnp.where(live, send_rows[0], -1).reshape(NX, 1, parts * slots // NX)
    col_blocks = (own_rows + parts * slots) // tiles.shape[2]
    table = tile_order(tile_rows[0], tile_cols[0], col_blocks)
    grad_scale = float(own_rows * lax.axis_size("node")) ** (-0.5)
    hidden, grad_features, totals = layer(
        table, picks, features[0], tiles[0], w_neigh, w_self, cotangent[0], grad_scale
    )
    return hidden[None], grad_features[None], totals[0], totals[1]


def solution(mesh):
    placed = (
        P("node", "feat", None),
        P("node", None, None, None),
        P("node", None),
        P("node", None),
        P("node", None, None),
        P("node", None),
        P("feat", None),
        P("feat", None),
        P("node", "feat", None),
    )
    return jax.shard_map(
        per_device,
        mesh=mesh,
        in_specs=placed,
        out_specs=(
            P("node", "feat", None),
            P("node", "feat", None),
            P("feat", None),
            P("feat", None),
        ),
        check_vma=False,
    )
```

```python
import functools

import jax
import jax.numpy as jnp
from jax import lax
from jax.experimental import pallas as pl
from jax.experimental.pallas import tpu as pltpu
from jax.sharding import PartitionSpec as P

NX, NY, NZ, NC = 4, 4, 8, 2
NODES = NX * NZ * NC
GROUP = NZ * NC
X_ORDER = (2, 1, 3, 0)
MESH = pl.DeviceIdType.MESH
F32 = jnp.float32
BF16 = jnp.bfloat16
CONTRACT_FIRST = (((0,), (0,)), ((), ()))
CONTRACT_LAST = (((1,), (1,)), ((), ()))


def node_of(x, z, c):
    return (x * NZ + z) * NC + c


def remote(src, dst, send, recv, device):
    return pltpu.make_async_remote_copy(
        src_ref=src, dst_ref=dst, send_sem=send, recv_sem=recv, device_id=device, device_id_type=MESH
    )


def dot(a, b):
    return jnp.dot(a, b, preferred_element_type=F32)


def dot_last(a, b):
    return lax.dot_general(a, b, CONTRACT_LAST, preferred_element_type=F32)


def exchange_quarters(pieces):
    quarter = pieces[0].shape[1] // 4
    lane_quarter = lax.broadcasted_iota(jnp.int32, pieces[0].shape, 1) // quarter
    result = []
    for b in range(4):
        moved = pieces[b]
        for a in range(4):
            if a != b:
                rolled = pltpu.roll(pieces[a], ((a - b) % 4) * quarter, 1)
                moved = jnp.where(lane_quarter == a, rolled, moved)
        result.append(moved)
    return result


def tile_table(row_ref, col_ref, out_ref):
    count = row_ref.shape[1]
    upright = lax.broadcasted_iota(jnp.int32, (count, count), 0)
    across = lax.broadcasted_iota(jnp.int32, (count, count), 1)
    stand = lambda line: jnp.sum(jnp.where(upright == across, line, 0), axis=1, keepdims=True)
    column = lambda mask, value: jnp.sum(jnp.where(mask, value, 0), axis=0, keepdims=True)
    keys = row_ref[...], col_ref[...]
    stood = [stand(line) for line in keys]
    for t in range(2):
        line, post = keys[t], stood[t]
        before = (line < post) | ((line == post) & (across < upright))
        rank = jnp.sum(before.astype(jnp.int32), axis=1, keepdims=True)
        chosen = rank == across
        own = column(chosen, post)
        previous = column(rank == across - 1, post)
        results = (
            column(chosen, upright),
            column(chosen, stood[1 - t]),
            jnp.where((own == previous) & (across[:1] > 0), 1, 0),
            jnp.maximum(column(post <= across, 1) - 1, 0),
            jnp.minimum(column(post == across, 1), 1),
        )
        for i, result in enumerate(results):
            out_ref[t * 5 + i, :, pl.ds(0, count)] = result


def layer_kernel(
    scale,
    row_ref, col_ref, picks, feat_hbm, tiles_hbm, wn_hbm, ws_hbm, cot_hbm,
    hidden_hbm, gfeat_ref, total_neigh, total_self,
    feat, tiles, cot, weights, onehot, msg_out, msg_in, ext, running, agg_out, cols, pre, gate, hidden,
    back_out, back_in, own_term, other_term, core_in, x_out, x_in, y_out, y_in, z_out, z_in, z_sum,
    strip, rows, other, blocks, spread, acc,
    ret_out, ret_in, table_rows, table,
    load_sem, halo_send, halo_recv, self_send, self_recv, w_send, w_recv, wf_send, wf_recv, wc_send, wc_recv,
    agg_send, agg_recv, ba_send, ba_recv, bs_send, bs_recv, c_send, c_recv, x_send, x_recv, y_send, y_recv,
    z_send, z_recv, zg_send, zg_recv, xg_send, xg_recv, cg_send, cg_recv, ret_send, ret_recv,
):
    n = lax.axis_index("node")
    y = lax.axis_index("feat")
    x, z, c = lax.div(n, GROUP), lax.rem(lax.div(n, NC), NZ), lax.rem(n, NC)
    partner = {"node": node_of(x, z, 1 - c)}
    y_of = lambda d: lax.rem(y + d, NY)
    x_of = lambda d: lax.rem(x + d, NX)
    z_of = lambda d: lax.rem(z + d, NZ)
    c_of = lambda d: lax.rem(c + d, NC)
    y_peer = lambda d: {"feat": y_of(d)}
    x_peer = lambda d: {"node": node_of(x_of(d), z, c)}
    z_peer = lambda d: {"node": node_of(x, z_of(d), c)}
    width, own_rows = feat.shape
    share = own_rows // NY
    side = tiles.shape[1]
    n_tiles = tiles.shape[0]
    own_blocks = own_rows // side
    lanes = GROUP * 32
    hid = gate.shape[1]
    xr, zc = width // NX, hid // NZ
    offsets = [(dx, dz, dc) for dx in X_ORDER for dz in range(NZ) for dc in range(NC) if dx or dz or dc]

    started, due = [], {}

    def start(cp):
        cp.start()
        started.append(cp)
        due[id(cp)] = cp.wait_recv
        return cp

    def arrive(copies):
        for cp in copies:
            due.pop(id(cp))()

    barrier = pltpu.get_barrier_semaphore()
    for dx, dz, dc in offsets:
        pl.semaphore_signal(
            barrier, inc=1, device_id={"node": node_of(x_of(dx), z_of(dz), c_of(dc))}, device_id_type=MESH
        )
    for d in range(1, NY):
        pl.semaphore_signal(barrier, inc=1, device_id=y_peer(d), device_id_type=MESH)

    loads = [
        pltpu.make_async_copy(feat_hbm, feat, load_sem.at[0]),
        pltpu.make_async_copy(wn_hbm, weights.at[0, y], load_sem.at[1]),
        pltpu.make_async_copy(ws_hbm, weights.at[1, y], load_sem.at[2]),
        pltpu.make_async_copy(tiles_hbm, tiles, load_sem.at[3]),
        pltpu.make_async_copy(cot_hbm, cot, load_sem.at[4]),
    ]
    for load in loads:
        load.start()
    loads[0].wait()
    msg_in[n] = jnp.zeros(msg_in.shape[1:], BF16)

    def pick(dx):
        part = x_of(dx)
        wanted = picks[part]
        ids = lax.broadcasted_iota(jnp.int32, (own_rows, lanes), 0)
        onehot[part] = jnp.where(ids == wanted, 1.0, 0.0).astype(BF16)
        picked = dot(feat[...], onehot[part])
        for b in range(lanes // side):
            block = picked[:, b * side:(b + 1) * side]
            height = width // 4
            moved = exchange_quarters([block[a * height:(a + 1) * height] for a in range(4)])
            for p in range(4):
                msg_out[part * GROUP + b * 4 + p] = moved[p].astype(BF16)

    def halo_start(dx, out, into, send, recv):
        for dz in range(NZ):
            for dc in range(NC):
                if dx or dz or dc:
                    o = (dx * NZ + dz) * NC + dc
                    peer = node_of(x_of(dx), z_of(dz), c_of(dc))
                    cp = remote(out.at[peer], into.at[n], send.at[o], recv.at[o], {"node": peer})
                    cp.start()
                    started.append(cp)
        due[id(into), dx] = functools.partial(halo_arrive, dx, out, into, send, recv)

    def halo_arrive(dx, out, into, send, recv):
        for dz in range(NZ):
            for dc in range(NC):
                if dx or dz or dc:
                    o = (dx * NZ + dz) * NC + dc
                    src = node_of(x_of(NX - dx), z_of(NZ - dz), c_of(NC - dc))
                    remote(out.at[src], into.at[src], send.at[o], recv.at[o], {"node": src}).wait_recv()

    pick(X_ORDER[0])
    pl.semaphore_wait(barrier, len(offsets) + NY - 1)
    halo_start(X_ORDER[0], msg_out, msg_in, halo_send, halo_recv)
    loads[1].wait()
    loads[2].wait()
    w_right = remote(weights.at[c, y], weights.at[c, y], w_send.at[0], w_recv.at[0], y_peer(1))
    w_left = remote(weights.at[c, y], weights.at[c, y], w_send.at[1], w_recv.at[1], y_peer(NY - 1))
    start(w_right)
    start(w_left)
    selfs = []
    for d in range(1, NY):
        q = y_of(d)
        cp = remote(
            feat_hbm.at[:, pl.ds(pl.multiple_of(q * share, share), share)], cols.at[1, y],
            self_send.at[d - 1], self_recv.at[d - 1], y_peer(d),
        )
        selfs.append(start(cp))
    cols[1, y] = feat[:, pl.ds(pl.multiple_of(y * share, share), share)]
    for dx in X_ORDER[1:]:
        pick(dx)
        halo_start(dx, msg_out, msg_in, halo_send, halo_recv)

    half = width // 2
    low, high = pl.ds(0, half), pl.ds(half, half)
    left_id, right_id, far_id = y_of(NY - 1), y_of(1), y_of(2)
    arrive([w_right])
    w_far_right = remote(
        weights.at[c, left_id, low], weights.at[c, left_id, low], wf_send.at[0], wf_recv.at[0], y_peer(1)
    )
    start(w_far_right)
    arrive([w_left])
    w_far_left = remote(
        weights.at[c, right_id, high], weights.at[c, right_id, high], wf_send.at[1], wf_recv.at[1], y_peer(NY - 1)
    )
    start(w_far_left)
    w_core = []
    for i, q in enumerate((left_id, right_id, far_id)):
        if i == 2:
            arrive([w_far_right])
            arrive([w_far_left])
        cp = remote(weights.at[c, q], weights.at[c, q], wc_send.at[i], wc_recv.at[i], partner)
        w_core.append(start(cp))

    tile_table(row_ref, col_ref, table_rows)
    table_copy = pltpu.make_async_copy(table_rows, table, load_sem.at[6])
    table_copy.start()
    for b in range(own_blocks):
        ext[b] = feat[:, b * side:(b + 1) * side]
    loads[3].wait()
    table_copy.wait()
    height = width // 4

    def unpack(source, first):
        moved = exchange_quarters([source[first + p].astype(F32) for p in range(4)])
        return jnp.concatenate([piece.astype(BF16) for piece in moved], axis=0)

    for dx in X_ORDER:
        due.pop((id(msg_in), dx))()
        part = x_of(NX - dx)
        for b in range(GROUP // 4):
            ext[own_blocks + part * (GROUP // 4) + b] = unpack(msg_in, part * GROUP + b * 4)

    unroll = 4

    def aggregate(i, total):
        for u in range(unroll):
            s = i * unroll + u
            total = total * table[2, 0, s].astype(F32) + dot_last(ext[table[1, 0, s]], tiles[table[0, 0, s]])
            running[s] = total.astype(BF16)
        return total

    lax.fori_loop(0, n_tiles // unroll, aggregate, jnp.zeros((width, side), F32))
    per = own_blocks // NY
    for r in range(own_blocks):
        agg_out[r // per, :, (r % per) * side:(r % per + 1) * side] = running[table[3, 0, r]]
    aggs = []
    for d in range(1, NY):
        cp = remote(agg_out.at[y_of(d)], cols.at[0, y], agg_send.at[d - 1], agg_recv.at[d - 1], y_peer(d))
        aggs.append(start(cp))
    cols[0, y] = agg_out[y]

    arrive(selfs)
    arrive(w_core)
    strips = 4
    wide = hid // strips

    def self_part(i, carry):
        at = pl.ds(pl.multiple_of(i * wide, wide), wide)
        left = cols[1].reshape(NY * width, share)
        right = weights[1, :, :, at].reshape(NY * width, wide)
        pre[:, at] = lax.dot_general(left, right, CONTRACT_FIRST, preferred_element_type=F32)
        return carry

    lax.fori_loop(0, strips, self_part, 0)
    loads[4].wait()
    arrive(aggs)

    def neigh_part(i, carry):
        at = pl.ds(pl.multiple_of(i * wide, wide), wide)
        left = cols[0].reshape(NY * width, share)
        right = weights[0, :, :, at].reshape(NY * width, wide)
        value = pre[:, at] + lax.dot_general(left, right, CONTRACT_FIRST, preferred_element_type=F32)
        sig = jax.nn.sigmoid(value)
        hidden[:, at] = (value * sig).astype(BF16)
        gate[:, at] = (cot[:, at].astype(F32) * sig * (1.0 + value * (1.0 - sig))).astype(BF16)
        return carry

    lax.fori_loop(0, strips, neigh_part, 0)
    store_hidden = pltpu.make_async_copy(hidden, hidden_hbm, load_sem.at[5])
    store_hidden.start()

    backs = []
    for d in range(1, NY):
        q = y_of(d)
        back_out[0, q] = dot_last(weights[0, q], gate[...]).astype(BF16)
        cp = remote(back_out.at[0, q], back_in.at[0, y], ba_send.at[d - 1], ba_recv.at[d - 1], y_peer(d))
        backs.append(start(cp))
    back_in[0, y] = dot_last(weights[0, y], gate[...]).astype(BF16)

    y_order = (1, 2, 3, 0)
    swaps, xs, ys = {}, {}, []
    for d in y_order:
        q = y_of(d)
        other_term[q] = dot(cols[1 - c, q], gate[...]).astype(BF16)
        swaps[d] = start(remote(other_term.at[q], core_in.at[q], c_send.at[d], c_recv.at[d], partner))
    for d in y_order:
        q = y_of(d)
        term = dot(cols[c, q], gate[...])
        arrive([swaps[d]])
        own_term[q] = term + core_in[q].astype(F32)
        xs[d] = []
        for e in range(1, NX):
            at = pl.ds(pl.multiple_of(x_of(e) * xr, xr), xr)
            x_out[e - 1, q] = own_term[q, at].astype(BF16)
            k = d * (NX - 1) + e - 1
            xs[d].append(
                start(remote(x_out.at[e - 1, q], x_in.at[e - 1, q], x_send.at[k], x_recv.at[k], x_peer(e)))
            )
    back_selfs = []
    for d in range(1, NY):
        q = y_of(d)
        back_out[1, q] = dot_last(weights[1, q], gate[...]).astype(BF16)
        cp = remote(back_out.at[1, q], back_in.at[1, y], bs_send.at[d - 1], bs_recv.at[d - 1], y_peer(d))
        back_selfs.append(start(cp))
    back_in[1, y] = dot_last(weights[1, y], gate[...]).astype(BF16)

    def sum_over_x(d):
        q = y_of(d)
        arrive(xs[d])
        mine = own_term[q, pl.ds(pl.multiple_of(x * xr, xr), xr)]
        for e in range(1, NX):
            mine = mine + x_in[e - 1, q].astype(F32)
        return mine

    def send_over_y(d):
        y_out[d - 1] = sum_over_x(d).astype(BF16)
        ys.append(start(remote(y_out.at[d - 1], y_in.at[d - 1], y_send.at[d - 1], y_recv.at[d - 1], y_peer(d))))

    arrive(backs)
    for r in range(own_blocks):
        blocks[r] = back_in[0, r // per, :, (r % per) * side:(r % per + 1) * side]

    def spread_back(i, total):
        for u in range(unroll):
            s = i * unroll + u
            total = total * table[7, 0, s].astype(F32) + dot(blocks[table[6, 0, s]], tiles[table[5, 0, s]])
            spread[s] = total
        return total

    lax.fori_loop(0, n_tiles // unroll, spread_back, jnp.zeros((width, side), F32))

    def send_back(dx):
        part = x_of(dx)
        for b in range(GROUP // 4):
            col = own_blocks + part * (GROUP // 4) + b
            block = spread[table[8, 0, col]] * table[9, 0, col].astype(F32)
            moved = exchange_quarters([block[a * height:(a + 1) * height] for a in range(4)])
            for p in range(4):
                ret_out[part * GROUP + b * 4 + p] = moved[p].astype(BF16)
        halo_start(dx, ret_out, ret_in, ret_send, ret_recv)

    def scatter(dx):
        due.pop((id(ret_in), dx))()
        part = x_of(NX - dx)
        came = jnp.concatenate(
            [unpack(ret_in, part * GROUP + b * 4) for b in range(GROUP // 4)], axis=1
        )
        acc[...] += dot_last(came, onehot[part])

    ret_in[n] = jnp.zeros(ret_in.shape[1:], BF16)
    send_back(X_ORDER[0])
    send_over_y(1)
    send_over_y(2)
    send_back(X_ORDER[1])
    send_over_y(3)
    mine = sum_over_x(0)
    arrive(ys)
    for d in range(1, NY):
        mine = mine + y_in[d - 1].astype(F32)
    for q in range(NZ):
        z_out[q] = mine[:, q * zc:(q + 1) * zc].astype(BF16)
    zs = []
    for d in range(1, NZ):
        cp = remote(z_out.at[z_of(d)], z_in.at[d - 1], z_send.at[d - 1], z_recv.at[d - 1], z_peer(d))
        zs.append(start(cp))
    send_back(X_ORDER[2])
    arrive(back_selfs)
    for b in range(own_blocks):
        at = slice(b * side, (b + 1) * side)
        inner = slice((b % per) * side, (b % per + 1) * side)
        acc[:, at] = spread[table[8, 0, b]] * table[9, 0, b].astype(F32) + back_in[1, b // per, :, inner].astype(F32)
    arrive(zs)
    mine = z_out[z].astype(F32)
    for d in range(1, NZ):
        mine = mine + z_in[d - 1].astype(F32)
    z_sum[...] = mine.astype(BF16)
    zgs = []
    for d in range(1, NZ):
        cp = remote(z_sum, strip.at[z], zg_send.at[d - 1], zg_recv.at[d - 1], z_peer(d))
        zgs.append(start(cp))
    strip[z] = z_sum[...]
    send_back(X_ORDER[3])
    scatter(X_ORDER[0])
    arrive(zgs)
    xgs = []
    for d in range(1, NX):
        cp = remote(strip, rows.at[x], xg_send.at[d - 1], xg_recv.at[d - 1], x_peer(d))
        xgs.append(start(cp))
    rows[x] = strip[...]
    scatter(X_ORDER[1])
    arrive(xgs)
    last = start(remote(rows, other, cg_send.at[0], cg_recv.at[0], partner))
    for dx in X_ORDER[2:]:
        scatter(dx)
    gfeat_ref[...] = acc[...].astype(BF16)
    arrive([last])
    for a in range(NX):
        for b in range(NZ):
            ra, cb = slice(a * xr, (a + 1) * xr), slice(b * zc, (b + 1) * zc)
            mine, theirs = rows[a, b].astype(F32) * scale, other[a, b].astype(F32) * scale
            total_neigh[ra, cb] = jnp.where(c == 0, mine, theirs)
            total_self[ra, cb] = jnp.where(c == 0, theirs, mine)
    store_hidden.wait()
    for cp in started:
        cp.wait_send()


def layer(row_ids, col_ids, picks, feat, tiles, wn, ws, cot, scale):
    width, own_rows = feat.shape
    n_tiles, side, _ = tiles.shape
    share, hid = cot.shape
    xr, zc = width // NX, hid // NZ
    own_blocks = own_rows // side
    lanes = own_rows // NX
    height = width // 4
    vmem = pltpu.VMEM
    dma = lambda k: pltpu.SemaphoreType.DMA((k,))
    any_space = pl.BlockSpec(memory_space=pl.ANY)
    in_vmem = pl.BlockSpec(memory_space=pltpu.VMEM)
    return pl.pallas_call(
        functools.partial(layer_kernel, scale),
        out_shape=(
            jax.ShapeDtypeStruct((share, hid), BF16),
            jax.ShapeDtypeStruct((width, own_rows), BF16),
            jax.ShapeDtypeStruct((width, hid), F32),
            jax.ShapeDtypeStruct((width, hid), F32),
        ),
        in_specs=[in_vmem] * 3 + [any_space] * 5,
        out_specs=(any_space, in_vmem, in_vmem, in_vmem),
        scratch_shapes=[
            vmem((width, own_rows), BF16),
            vmem((n_tiles, side, side), BF16),
            vmem((share, hid), BF16),
            vmem((2, NY, width, hid), BF16),
            vmem((NX, own_rows, lanes), BF16),
            vmem((NODES, height, side), BF16),
            vmem((NODES, height, side), BF16),
            vmem((2 * own_blocks, width, side), BF16),
            vmem((n_tiles, width, side), BF16),
            vmem((NY, width, share), BF16),
            vmem((2, NY, width, share), BF16),
            vmem((share, hid), F32),
            vmem((share, hid), BF16),
            vmem((share, hid), BF16),
            vmem((2, NY, width, share), BF16),
            vmem((2, NY, width, share), BF16),
            vmem((NY, width, hid), F32),
            vmem((NY, width, hid), BF16),
            vmem((NY, width, hid), BF16),
            vmem((NX - 1, NY, xr, hid), BF16),
            vmem((NX - 1, NY, xr, hid), BF16),
            vmem((NY - 1, xr, hid), BF16),
            vmem((NY - 1, xr, hid), BF16),
            vmem((NZ, xr, zc), BF16),
            vmem((NZ - 1, xr, zc), BF16),
            vmem((xr, zc), BF16),
            vmem((NZ, xr, zc), BF16),
            vmem((NX, NZ, xr, zc), BF16),
            vmem((NX, NZ, xr, zc), BF16),
            vmem((own_blocks, width, side), BF16),
            vmem((n_tiles, width, side), F32),
            vmem((width, own_rows), F32),
            vmem((NODES, height, side), BF16),
            vmem((NODES, height, side), BF16),
            vmem((10, 1, 128), jnp.int32),
            pltpu.SMEM((10, 1, 128), jnp.int32),
            dma(7), dma(NODES), dma(NODES), dma(3), dma(3), dma(2), dma(2), dma(2), dma(2), dma(3), dma(3),
            dma(3), dma(3), dma(3), dma(3), dma(3), dma(3), dma(4), dma(4), dma(12), dma(12), dma(3), dma(3),
            dma(7), dma(7), dma(7), dma(7), dma(3), dma(3), dma(1), dma(1), dma(NODES), dma(NODES),
        ],
        compiler_params=pltpu.CompilerParams(
            collective_id=0, has_side_effects=True, vmem_limit_bytes=60 << 20
        ),
        name="sage_layer",
    )(row_ids, col_ids, picks, feat, tiles, wn, ws, cot)


def per_device(
    features, tiles, tile_rows, tile_cols, send_rows, send_count, w_neigh, w_self, cotangent
):
    own_rows = features.shape[2]
    parts, slots = send_rows.shape[1:]
    live = lax.broadcasted_iota(jnp.int32, (parts, slots), 1) < send_count[0][:, None]
    picks = jnp.where(live, send_rows[0], -1).reshape(NX, 1, parts * slots // NX)
    grad_scale = float(own_rows * lax.axis_size("node")) ** (-0.5)
    hidden, grad_features, total_neigh, total_self = layer(
        tile_rows, tile_cols, picks, features[0], tiles[0], w_neigh, w_self, cotangent[0], grad_scale
    )
    return hidden[None], grad_features[None], total_neigh, total_self


def solution(mesh):
    placed = (
        P("node", "feat", None),
        P("node", None, None, None),
        P("node", None),
        P("node", None),
        P("node", None, None),
        P("node", None),
        P("feat", None),
        P("feat", None),
        P("node", "feat", None),
    )
    return jax.shard_map(
        per_device,
        mesh=mesh,
        in_specs=placed,
        out_specs=(
            P("node", "feat", None),
            P("node", "feat", None),
            P("feat", None),
            P("feat", None),
        ),
        check_vma=False,
    )
```

```python
import functools

import jax
import jax.numpy as jnp
from jax import lax
from jax.experimental import pallas as pl
from jax.experimental.pallas import tpu as pltpu
from jax.sharding import PartitionSpec as P

NX, NY, NZ, NC = 4, 4, 8, 2
NODES = NX * NZ * NC
GROUP = NZ * NC
X_ORDER = (2, 1, 3, 0)
RETURN_ORDER = (0, 2, 1, 3)
STRIPS = 4
MESH = pl.DeviceIdType.MESH
F32 = jnp.float32
BF16 = jnp.bfloat16
CONTRACT_FIRST = (((0,), (0,)), ((), ()))
CONTRACT_LAST = (((1,), (1,)), ((), ()))


def node_of(x, z, c):
    return (x * NZ + z) * NC + c


def remote(src, dst, send, recv, device):
    return pltpu.make_async_remote_copy(
        src_ref=src, dst_ref=dst, send_sem=send, recv_sem=recv, device_id=device, device_id_type=MESH
    )


def dot(a, b):
    return jnp.dot(a, b, preferred_element_type=F32)


def dot_last(a, b):
    return lax.dot_general(a, b, CONTRACT_LAST, preferred_element_type=F32)


def exchange_quarters(pieces):
    quarter = pieces[0].shape[1] // 4
    lane_quarter = lax.broadcasted_iota(jnp.int32, pieces[0].shape, 1) // quarter
    result = []
    for b in range(4):
        moved = pieces[b]
        for a in range(4):
            if a != b:
                rolled = pltpu.roll(pieces[a], ((a - b) % 4) * quarter, 1)
                moved = jnp.where(lane_quarter == a, rolled, moved)
        result.append(moved)
    return result


def tile_table(row_ref, col_ref, out_ref):
    count = row_ref.shape[1]
    upright = lax.broadcasted_iota(jnp.int32, (count, count), 0)
    across = lax.broadcasted_iota(jnp.int32, (count, count), 1)
    stand = lambda line: jnp.sum(jnp.where(upright == across, line, 0), axis=1, keepdims=True)
    column = lambda mask, value: jnp.sum(jnp.where(mask, value, 0), axis=0, keepdims=True)
    keys = row_ref[...], col_ref[...]
    stood = [stand(line) for line in keys]
    for t in range(2):
        line, post = keys[t], stood[t]
        before = (line < post) | ((line == post) & (across < upright))
        rank = jnp.sum(before.astype(jnp.int32), axis=1, keepdims=True)
        chosen = rank == across
        own = column(chosen, post)
        previous = column(rank == across - 1, post)
        results = (
            column(chosen, upright),
            column(chosen, stood[1 - t]),
            jnp.where((own == previous) & (across[:1] > 0), 1, 0),
            jnp.maximum(column(post <= across, 1) - 1, 0),
            jnp.minimum(column(post == across, 1), 1),
        )
        for i, result in enumerate(results):
            out_ref[t * 5 + i, :, pl.ds(0, count)] = result


def layer_kernel(
    scale,
    row_ref, col_ref, sends, counts, feat_hbm, tiles_hbm, wn_hbm, ws_hbm, cot_hbm,
    hidden_hbm, gfeat_ref, total_neigh, total_self,
    feat, tiles, cot, weights, onehot, msg_out, msg_in, ext, running, agg_out, cols, pre, gate, hidden,
    back_out, back_in, own_term, own_sum, other_term, core_in, x_out, x_in, y_out, y_in,
    first_y_out, first_y_in, last_x_out, last_x_in, z_out, z_in, z_sum,
    strip, rows, other, blocks, spread, acc,
    ret_out, ret_in, table_rows, table,
    load_sem, halo_send, halo_recv, self_send, self_recv, w_send, w_recv, wf_send, wf_recv, wc_send, wc_recv,
    agg_send, agg_recv, ba_send, ba_recv, bs_send, bs_recv, c_send, c_recv, x_send, x_recv, y_send, y_recv,
    z_send, z_recv, zg_send, zg_recv, xg_send, xg_recv, cg_send, cg_recv, ret_send, ret_recv,
):
    n = lax.axis_index("node")
    y = lax.axis_index("feat")
    x, z, c = lax.div(n, GROUP), lax.rem(lax.div(n, NC), NZ), lax.rem(n, NC)
    partner = {"node": node_of(x, z, 1 - c)}
    y_of = lambda d: lax.rem(y + d, NY)
    x_of = lambda d: lax.rem(x + d, NX)
    z_of = lambda d: lax.rem(z + d, NZ)
    c_of = lambda d: lax.rem(c + d, NC)
    y_peer = lambda d: {"feat": y_of(d)}
    x_peer = lambda d: {"node": node_of(x_of(d), z, c)}
    z_peer = lambda d: {"node": node_of(x, z_of(d), c)}
    width, own_rows = feat.shape
    share = own_rows // NY
    side = tiles.shape[1]
    n_tiles = tiles.shape[0]
    own_blocks = own_rows // side
    slots = sends.shape[1]
    lanes = GROUP * slots
    hid = gate.shape[1]
    xr, zc = width // NX, hid // NZ
    offsets = [(dx, dz, dc) for dx in X_ORDER for dz in range(NZ) for dc in range(NC) if dx or dz or dc]

    started, due = [], {}

    def start(cp):
        cp.start()
        started.append(cp)
        due[id(cp)] = cp.wait_recv
        return cp

    def arrive(copies):
        for cp in copies:
            due.pop(id(cp))()

    barrier = pltpu.get_barrier_semaphore()
    for dx, dz, dc in offsets:
        pl.semaphore_signal(
            barrier, inc=1, device_id={"node": node_of(x_of(dx), z_of(dz), c_of(dc))}, device_id_type=MESH
        )
    for d in range(1, NY):
        pl.semaphore_signal(barrier, inc=1, device_id=y_peer(d), device_id_type=MESH)

    loads = [
        pltpu.make_async_copy(feat_hbm, feat, load_sem.at[0]),
        pltpu.make_async_copy(wn_hbm, weights.at[0, y], load_sem.at[1]),
        pltpu.make_async_copy(ws_hbm, weights.at[1, y], load_sem.at[2]),
        pltpu.make_async_copy(tiles_hbm, tiles, load_sem.at[3]),
        pltpu.make_async_copy(cot_hbm, cot, load_sem.at[4]),
    ]
    for load in loads:
        load.start()
    loads[0].wait()
    msg_in[n] = jnp.zeros(msg_in.shape[1:], BF16)

    def pick(dx):
        part = x_of(dx)
        near = pl.ds(pl.multiple_of(part * GROUP, GROUP), GROUP)
        slot = lax.broadcasted_iota(jnp.int32, (GROUP, slots), 1)
        live = jnp.where(slot < counts[near], sends[near], -1)
        wanted = jnp.concatenate([live[k:k + 1] for k in range(GROUP)], axis=1)
        ids = lax.broadcasted_iota(jnp.int32, (own_rows, lanes), 0)
        onehot[part] = jnp.where(ids == wanted, 1.0, 0.0).astype(BF16)
        picked = dot(feat[...], onehot[part])
        for b in range(lanes // side):
            block = picked[:, b * side:(b + 1) * side]
            height = width // 4
            moved = exchange_quarters([block[a * height:(a + 1) * height] for a in range(4)])
            for p in range(4):
                msg_out[part * GROUP + b * 4 + p] = moved[p].astype(BF16)

    def halo_start(dx, out, into, send, recv):
        for dz in range(NZ):
            for dc in range(NC):
                if dx or dz or dc:
                    o = (dx * NZ + dz) * NC + dc
                    peer = node_of(x_of(dx), z_of(dz), c_of(dc))
                    cp = remote(out.at[peer], into.at[n], send.at[o], recv.at[o], {"node": peer})
                    cp.start()
                    started.append(cp)
        due[id(into), dx] = functools.partial(halo_arrive, dx, out, into, send, recv)

    def halo_arrive(dx, out, into, send, recv):
        for dz in range(NZ):
            for dc in range(NC):
                if dx or dz or dc:
                    o = (dx * NZ + dz) * NC + dc
                    src = node_of(x_of(NX - dx), z_of(NZ - dz), c_of(NC - dc))
                    remote(out.at[src], into.at[src], send.at[o], recv.at[o], {"node": src}).wait_recv()

    pick(X_ORDER[0])
    pl.semaphore_wait(barrier, len(offsets) + NY - 1)
    halo_start(X_ORDER[0], msg_out, msg_in, halo_send, halo_recv)
    loads[1].wait()
    loads[2].wait()
    w_right = remote(weights.at[c, y], weights.at[c, y], w_send.at[0], w_recv.at[0], y_peer(1))
    w_left = remote(weights.at[c, y], weights.at[c, y], w_send.at[1], w_recv.at[1], y_peer(NY - 1))
    start(w_right)
    start(w_left)
    selfs = []
    for d in range(1, NY):
        q = y_of(d)
        cp = remote(
            feat_hbm.at[:, pl.ds(pl.multiple_of(q * share, share), share)], cols.at[1, y],
            self_send.at[d - 1], self_recv.at[d - 1], y_peer(d),
        )
        selfs.append(start(cp))
    cols[1, y] = feat[:, pl.ds(pl.multiple_of(y * share, share), share)]
    for dx in X_ORDER[1:]:
        pick(dx)
        halo_start(dx, msg_out, msg_in, halo_send, halo_recv)

    half = width // 2
    low, high = pl.ds(0, half), pl.ds(half, half)
    left_id, right_id, far_id = y_of(NY - 1), y_of(1), y_of(2)
    arrive([w_right])
    w_far_right = remote(
        weights.at[c, left_id, low], weights.at[c, left_id, low], wf_send.at[0], wf_recv.at[0], y_peer(1)
    )
    start(w_far_right)
    arrive([w_left])
    w_far_left = remote(
        weights.at[c, right_id, high], weights.at[c, right_id, high], wf_send.at[1], wf_recv.at[1], y_peer(NY - 1)
    )
    start(w_far_left)
    w_core = []
    for i, q in enumerate((left_id, right_id, far_id)):
        if i == 2:
            arrive([w_far_right])
            arrive([w_far_left])
        cp = remote(weights.at[c, q], weights.at[c, q], wc_send.at[i], wc_recv.at[i], partner)
        w_core.append(start(cp))

    tile_table(row_ref, col_ref, table_rows)
    table_copy = pltpu.make_async_copy(table_rows, table, load_sem.at[6])
    table_copy.start()
    for b in range(own_blocks):
        ext[b] = feat[:, b * side:(b + 1) * side]
    loads[3].wait()
    table_copy.wait()
    height = width // 4

    def unpack(source, first):
        moved = exchange_quarters([source[first + p].astype(F32) for p in range(4)])
        return jnp.concatenate([piece.astype(BF16) for piece in moved], axis=0)

    for dx in X_ORDER:
        due.pop((id(msg_in), dx))()
        part = x_of(NX - dx)
        for b in range(GROUP // 4):
            ext[own_blocks + part * (GROUP // 4) + b] = unpack(msg_in, part * GROUP + b * 4)

    unroll = 4

    def aggregate(i, total):
        for u in range(unroll):
            s = i * unroll + u
            total = total * table[2, 0, s].astype(F32) + dot_last(ext[table[1, 0, s]], tiles[table[0, 0, s]])
            running[s] = total.astype(BF16)
        return total

    lax.fori_loop(0, n_tiles // unroll, aggregate, jnp.zeros((width, side), F32))
    per = own_blocks // NY
    for r in range(own_blocks):
        agg_out[r // per, :, (r % per) * side:(r % per + 1) * side] = running[table[3, 0, r]]
    aggs = []
    for d in range(1, NY):
        cp = remote(agg_out.at[y_of(d)], cols.at[0, y], agg_send.at[d - 1], agg_recv.at[d - 1], y_peer(d))
        aggs.append(start(cp))
    cols[0, y] = agg_out[y]

    arrive(selfs)
    arrive(w_core)
    strips = STRIPS
    wide = hid // strips

    def self_part(i, carry):
        at = pl.ds(pl.multiple_of(i * wide, wide), wide)
        left = cols[1].reshape(NY * width, share)
        right = weights[1, :, :, at].reshape(NY * width, wide)
        pre[:, at] = lax.dot_general(left, right, CONTRACT_FIRST, preferred_element_type=F32)
        return carry

    lax.fori_loop(0, strips, self_part, 0)
    loads[4].wait()
    arrive(aggs)

    def neigh_part(i, carry):
        at = pl.ds(pl.multiple_of(i * wide, wide), wide)
        left = cols[0].reshape(NY * width, share)
        right = weights[0, :, :, at].reshape(NY * width, wide)
        value = pre[:, at] + lax.dot_general(left, right, CONTRACT_FIRST, preferred_element_type=F32)
        sig = jax.nn.sigmoid(value)
        hidden[:, at] = (value * sig).astype(BF16)
        gate[:, at] = (cot[:, at].astype(F32) * sig * (1.0 + value * (1.0 - sig))).astype(BF16)
        return carry

    lax.fori_loop(0, strips, neigh_part, 0)
    store_hidden = pltpu.make_async_copy(hidden, hidden_hbm, load_sem.at[5])
    store_hidden.start()

    backs = []
    for d in range(1, NY):
        q = y_of(d)
        back_out[0, q] = dot_last(weights[0, q], gate[...]).astype(BF16)
        cp = remote(back_out.at[0, q], back_in.at[0, y], ba_send.at[d - 1], ba_recv.at[d - 1], y_peer(d))
        backs.append(start(cp))
    back_in[0, y] = dot_last(weights[0, y], gate[...]).astype(BF16)

    swaps, xs, ys = [], [], []
    for t in range(strips):
        at = slice(t * wide, (t + 1) * wide)
        term = dot(cols[1 - c].reshape(NY * width, share), gate[:, at])
        other_term[t] = term.astype(BF16).reshape(NY, width, wide)
        swaps.append(start(remote(other_term.at[t], core_in.at[t], c_send.at[t], c_recv.at[t], partner)))

    def sum_over_cores(t):
        at = slice(t * wide, (t + 1) * wide)
        term = dot(cols[c].reshape(NY * width, share), gate[:, at]).reshape(NY, width, wide)
        arrive([swaps[t]])
        own_term[t] = term + core_in[t].astype(F32)

    my_rows = pl.ds(pl.multiple_of(x * xr, xr), xr)
    for t in range(strips - 1):
        sum_over_cores(t)
        xs.append([])
        for d in range(1, NX):
            x_out[t, d - 1] = own_term[t, :, pl.ds(pl.multiple_of(x_of(d) * xr, xr), xr)].astype(BF16)
            k = t * (NX - 1) + d - 1
            cp = remote(x_out.at[t, d - 1], x_in.at[t, d - 1], x_send.at[k], x_recv.at[k], x_peer(d))
            xs[t].append(start(cp))
    sum_over_cores(strips - 1)
    first_ys = []
    for d in range(1, NY):
        first_y_out[d - 1] = own_term[strips - 1, y_of(d)].astype(BF16)
        k = (strips - 1) * (NY - 1) + d - 1
        cp = remote(first_y_out.at[d - 1], first_y_in.at[d - 1], y_send.at[k], y_recv.at[k], y_peer(d))
        first_ys.append(start(cp))

    def x_to_y(t):
        arrive(xs[t])
        mine = own_term[t, :, my_rows]
        for d in range(1, NX):
            mine = mine + x_in[t, d - 1].astype(F32)
        own_sum[t] = mine
        ys.append([])
        for d in range(1, NY):
            y_out[t, d - 1] = own_sum[t, y_of(d)].astype(BF16)
            k = t * (NY - 1) + d - 1
            cp = remote(y_out.at[t, d - 1], y_in.at[t, d - 1], y_send.at[k], y_recv.at[k], y_peer(d))
            ys[t].append(start(cp))

    last_xs, xgs = [], []

    def y_to_x():
        arrive(first_ys)
        mine = own_term[strips - 1, y]
        for d in range(1, NY):
            mine = mine + first_y_in[d - 1].astype(F32)
        own_term[strips - 1, y] = mine
        for d in range(1, NX):
            rows_of = pl.ds(pl.multiple_of(x_of(d) * xr, xr), xr)
            last_x_out[d - 1] = own_term[strips - 1, y, rows_of].astype(BF16)
            k = (strips - 1) * (NX - 1) + d - 1
            cp = remote(last_x_out.at[d - 1], last_x_in.at[d - 1], x_send.at[k], x_recv.at[k], x_peer(d))
            last_xs.append(start(cp))

    for d in range(1, NY):
        back_out[1, y_of(d)] = dot_last(weights[1, y_of(d)], gate[...]).astype(BF16)
    back_in[1, y] = dot_last(weights[1, y], gate[...]).astype(BF16)

    per_strip = wide // zc
    maybe_started, lasts = [], []

    def sum_over_y(t):
        if t < strips - 1:
            arrive(ys[t])
            mine = own_sum[t, y]
            for d in range(1, NY):
                mine = mine + y_in[t, d - 1].astype(F32)
        else:
            arrive(last_xs)
            mine = own_term[t, y, my_rows]
            for d in range(1, NX):
                mine = mine + last_x_in[d - 1].astype(F32)
        for u in range(per_strip):
            piece = t * per_strip + u
            z_out[piece] = mine[:, u * zc:(u + 1) * zc].astype(BF16)
            k = lax.rem(piece - z + NZ - 1, NZ)
            cp = remote(z_out.at[piece], z_in.at[k], z_send.at[k], z_recv.at[k], {"node": node_of(x, piece, c)})
            pl.when(z != piece)(cp.start)
            maybe_started.append((z != piece, cp))

    def piece_copy(d):
        return remote(z_sum, strip.at[z], zg_send.at[d - 1], zg_recv.at[d - 1], z_peer(d))

    def sum_over_z(t):
        @pl.when(lax.div(z, per_strip) == t)
        def _():
            mine = z_out[z].astype(F32)
            for d in range(1, NZ):
                remote(z_out.at[z], z_in.at[d - 1], z_send.at[d - 1], z_recv.at[d - 1], z_peer(d)).wait_recv()
                mine = mine + z_in[d - 1].astype(F32)
            z_sum[...] = mine.astype(BF16)
            for d in range(1, NZ):
                piece_copy(d).start()
            strip[z] = z_sum[...]

    def gather_over_x(t):
        for u in range(per_strip):
            piece = t * per_strip + u
            k = lax.rem(z - piece + NZ - 1, NZ)
            cp = remote(z_sum, strip.at[piece], zg_send.at[k], zg_recv.at[k], {"node": node_of(x, piece, c)})
            pl.when(z != piece)(cp.wait_recv)
        pieces = pl.ds(t * per_strip, per_strip)
        xgs.append([])
        for d in range(1, NX):
            k = t * (NX - 1) + d - 1
            cp = remote(strip.at[pieces], rows.at[x, pieces], xg_send.at[k], xg_recv.at[k], x_peer(d))
            xgs[t].append(start(cp))
        rows[x, pieces] = strip[pieces]

    def gather_over_cores(t):
        arrive(xgs[t])
        pieces = pl.ds(t * per_strip, per_strip)
        cp = remote(rows.at[:, pieces], other.at[:, pieces], cg_send.at[t], cg_recv.at[t], partner)
        lasts.append(start(cp))

    arrive(backs)
    for r in range(own_blocks):
        blocks[r] = back_in[0, r // per, :, (r % per) * side:(r % per + 1) * side]

    def spread_back(i, total):
        for u in range(unroll):
            s = i * unroll + u
            total = total * table[7, 0, s].astype(F32) + dot(blocks[table[6, 0, s]], tiles[table[5, 0, s]])
            spread[s] = total
        return total

    lax.fori_loop(0, n_tiles // unroll, spread_back, jnp.zeros((width, side), F32))

    def send_back(dx):
        part = x_of(dx)
        for b in range(GROUP // 4):
            col = own_blocks + part * (GROUP // 4) + b
            block = spread[table[8, 0, col]] * table[9, 0, col].astype(F32)
            moved = exchange_quarters([block[a * height:(a + 1) * height] for a in range(4)])
            for p in range(4):
                ret_out[part * GROUP + b * 4 + p] = moved[p].astype(BF16)
        halo_start(dx, ret_out, ret_in, ret_send, ret_recv)

    def scatter(dx):
        due.pop((id(ret_in), dx))()
        part = x_of(NX - dx)
        came = jnp.concatenate(
            [unpack(ret_in, part * GROUP + b * 4) for b in range(GROUP // 4)], axis=1
        )
        acc[...] += dot_last(came, onehot[part])

    ret_in[n] = jnp.zeros(ret_in.shape[1:], BF16)
    x_to_y(0)
    send_back(RETURN_ORDER[0])
    send_back(RETURN_ORDER[1])
    send_back(RETURN_ORDER[2])
    send_back(RETURN_ORDER[3])
    for b in range(own_blocks):
        acc[:, b * side:(b + 1) * side] = spread[table[8, 0, b]] * table[9, 0, b].astype(F32)
    x_to_y(1)
    sum_over_y(0)
    x_to_y(2)
    y_to_x()
    sum_over_y(1)
    sum_over_y(2)
    sum_over_y(3)
    back_selfs = []
    for d in range(1, NY):
        cp = remote(
            back_out.at[1, y_of(d)], back_in.at[1, y], bs_send.at[d - 1], bs_recv.at[d - 1], y_peer(d)
        )
        back_selfs.append(start(cp))
    sum_over_z(0)
    sum_over_z(1)
    sum_over_z(2)
    sum_over_z(3)
    gather_over_x(0)
    gather_over_x(1)
    gather_over_x(2)
    gather_over_x(3)
    scatter(RETURN_ORDER[0])
    gather_over_cores(0)
    gather_over_cores(1)
    gather_over_cores(2)
    gather_over_cores(3)
    scatter(RETURN_ORDER[1])
    scatter(RETURN_ORDER[2])
    scatter(RETURN_ORDER[3])
    arrive(back_selfs)
    for q in range(NY):
        at = slice(q * share, (q + 1) * share)
        gfeat_ref[:, at] = (acc[:, at] + back_in[1, q].astype(F32)).astype(BF16)
    arrive(lasts)
    for a in range(NX):
        for b in range(NZ):
            ra, cb = slice(a * xr, (a + 1) * xr), slice(b * zc, (b + 1) * zc)
            mine, theirs = rows[a, b].astype(F32) * scale, other[a, b].astype(F32) * scale
            total_neigh[ra, cb] = jnp.where(c == 0, mine, theirs)
            total_self[ra, cb] = jnp.where(c == 0, theirs, mine)
    store_hidden.wait()
    for cp in started:
        cp.wait_send()
    for condition, cp in maybe_started:
        pl.when(condition)(cp.wait_send)
    for d in range(1, NZ):
        piece_copy(d).wait_send()


def layer(row_ids, col_ids, sends, counts, feat, tiles, wn, ws, cot, scale):
    width, own_rows = feat.shape
    n_tiles, side, _ = tiles.shape
    share, hid = cot.shape
    xr, zc = width // NX, hid // NZ
    own_blocks = own_rows // side
    lanes = own_rows // NX
    height = width // 4
    strips, wide = STRIPS, hid // STRIPS
    vmem = pltpu.VMEM
    dma = lambda k: pltpu.SemaphoreType.DMA((k,))
    any_space = pl.BlockSpec(memory_space=pl.ANY)
    in_vmem = pl.BlockSpec(memory_space=pltpu.VMEM)
    return pl.pallas_call(
        functools.partial(layer_kernel, scale),
        out_shape=(
            jax.ShapeDtypeStruct((share, hid), BF16),
            jax.ShapeDtypeStruct((width, own_rows), BF16),
            jax.ShapeDtypeStruct((width, hid), F32),
            jax.ShapeDtypeStruct((width, hid), F32),
        ),
        in_specs=[in_vmem] * 4 + [any_space] * 5,
        out_specs=(any_space, in_vmem, in_vmem, in_vmem),
        scratch_shapes=[
            vmem((width, own_rows), BF16),
            vmem((n_tiles, side, side), BF16),
            vmem((share, hid), BF16),
            vmem((2, NY, width, hid), BF16),
            vmem((NX, own_rows, lanes), BF16),
            vmem((NODES, height, side), BF16),
            vmem((NODES, height, side), BF16),
            vmem((2 * own_blocks, width, side), BF16),
            vmem((n_tiles, width, side), BF16),
            vmem((NY, width, share), BF16),
            vmem((2, NY, width, share), BF16),
            vmem((share, hid), F32),
            vmem((share, hid), BF16),
            vmem((share, hid), BF16),
            vmem((2, NY, width, share), BF16),
            vmem((2, NY, width, share), BF16),
            vmem((strips, NY, width, wide), F32),
            vmem((strips - 1, NY, xr, wide), F32),
            vmem((strips, NY, width, wide), BF16),
            vmem((strips, NY, width, wide), BF16),
            vmem((strips - 1, NX - 1, NY, xr, wide), BF16),
            vmem((strips - 1, NX - 1, NY, xr, wide), BF16),
            vmem((strips - 1, NY - 1, xr, wide), BF16),
            vmem((strips - 1, NY - 1, xr, wide), BF16),
            vmem((NY - 1, width, wide), BF16),
            vmem((NY - 1, width, wide), BF16),
            vmem((NX - 1, xr, wide), BF16),
            vmem((NX - 1, xr, wide), BF16),
            vmem((NZ, xr, zc), BF16),
            vmem((NZ, xr, zc), BF16),
            vmem((xr, zc), BF16),
            vmem((NZ, xr, zc), BF16),
            vmem((NX, NZ, xr, zc), BF16),
            vmem((NX, NZ, xr, zc), BF16),
            vmem((own_blocks, width, side), BF16),
            vmem((n_tiles, width, side), F32),
            vmem((width, own_rows), F32),
            vmem((NODES, height, side), BF16),
            vmem((NODES, height, side), BF16),
            vmem((10, 1, 128), jnp.int32),
            pltpu.SMEM((10, 1, 128), jnp.int32),
            dma(7), dma(NODES), dma(NODES), dma(3), dma(3), dma(2), dma(2), dma(2), dma(2), dma(3), dma(3),
            dma(3), dma(3), dma(3), dma(3), dma(3), dma(3), dma(4), dma(4), dma(12), dma(12), dma(12), dma(12),
            dma(8), dma(8), dma(8), dma(8), dma(12), dma(12), dma(4), dma(4), dma(NODES), dma(NODES),
        ],
        compiler_params=pltpu.CompilerParams(
            collective_id=0, has_side_effects=True, vmem_limit_bytes=60 << 20
        ),
        name="sage_layer",
    )(row_ids, col_ids, sends, counts, feat, tiles, wn, ws, cot)


def settle_kernel(*refs):
    count = (len(refs) - 1) // 3
    sources, targets, held, sems = refs[:count], refs[count:2 * count], refs[2 * count:-1], refs[-1]
    taken = [pltpu.make_async_copy(sources[i], held[i], sems.at[0, i]) for i in range(count)]
    put = [pltpu.make_async_copy(held[i], targets[i], sems.at[1, i]) for i in range(count)]
    for cp in taken:
        cp.start()
    for i in range(count):
        taken[i].wait()
        put[i].start()
    for cp in put:
        cp.wait()


def settle(arrays):
    spec = pl.BlockSpec(memory_space=pl.ANY)
    return pl.pallas_call(
        settle_kernel,
        out_shape=tuple(jax.ShapeDtypeStruct(a.shape, a.dtype) for a in arrays),
        in_specs=[spec] * len(arrays),
        out_specs=(spec,) * len(arrays),
        scratch_shapes=[pltpu.VMEM(a.shape, a.dtype) for a in arrays]
        + [pltpu.SemaphoreType.DMA((2, len(arrays)))],
        name="settle",
    )(*arrays)


def per_device(
    features, tiles, tile_rows, tile_cols, send_rows, send_count, w_neigh, w_self, cotangent
):
    own_rows = features.shape[2]
    grad_scale = float(own_rows * lax.axis_size("node")) ** (-0.5)
    results = layer(
        tile_rows, tile_cols, send_rows[0], send_count.reshape(-1, 1), features[0], tiles[0], w_neigh, w_self, cotangent[0], grad_scale
    )
    hidden, grad_features, total_neigh, total_self = settle(results)
    return hidden[None], grad_features[None], total_neigh, total_self


def solution(mesh):
    placed = (
        P("node", "feat", None),
        P("node", None, None, None),
        P("node", None),
        P("node", None),
        P("node", None, None),
        P("node", None),
        P("feat", None),
        P("feat", None),
        P("node", "feat", None),
    )
    return jax.shard_map(
        per_device,
        mesh=mesh,
        in_specs=placed,
        out_specs=(
            P("node", "feat", None),
            P("node", "feat", None),
            P("feat", None),
            P("feat", None),
        ),
        check_vma=False,
    )
```
